32 devices in a mesh: lon: 8 (over z, y), lat: 4 (over x, core).
Axes of the slice: x: 2, y: 2, z: 4, core: 2. Of those that a mesh axis runs over, the one named last changes fastest.
Arguments:
- zonal_wind: float32 [8, 128, 1024], P(None, 'lat', 'lon'), may hold values from -6 to 6
- meridional_wind: float32 [8, 128, 1024], P(None, 'lat', 'lon'), may hold values from -6 to 6
- theta_field: float32 [8, 128, 1024], P(None, 'lat', 'lon'), may hold values from -6 to 6
- pressure: float32 [8, 128, 1024], P(None, 'lat', 'lon'), may hold values from -6 to 6
- stiffness: float32 [8, 128, 1024], P(None, 'lat', 'lon'), may hold values from 1 to 8
Outputs:
- zonal_next: float32 [8, 128, 1024], P(None, 'lat', 'lon')
- meridional_next: float32 [8, 128, 1024], P(None, 'lat', 'lon')
- theta_next: float32 [8, 128, 1024], P(None, 'lat', 'lon')
- pressure_next: float32 [8, 128, 1024], P(None, 'lat', 'lon')
The draws below stay inside these ranges and needn't reach their ends.
All inputs are finite; a program needn't handle non-finite values.
Results may differ from the reference program's by a relative error of at most 0.00002.
Values sent between devices are 32-bit elements; how exact they have to be, the bound alone decides.
A program may use at most 64 MiB of HBM per device.

```python
import math
import jax
import jax.numpy as jnp

LEV = 8
SWEEPS = 3
NLAT = 128
NLON = 1024


def draw_pressure(key, part):
    noise_part = jnp.clip(jax.random.normal(key, (LEV, NLAT, NLON), jnp.float32), -6.0, 6.0)
    return noise_part


def block_scale(key, shape, shards, smallest, largest):
    loudness, own = 1.0, jax.random.fold_in(key, 6)
    for dim, blocks in shards:
        draws = jnp.exp(jax.random.uniform(jax.random.fold_in(own, dim), (blocks,), jnp.float32, smallest / len(shards), largest / len(shards)))
        loudness = loudness * jnp.repeat(draws, shape[dim] // blocks).reshape([-1 if axis == dim else 1 for axis in range(len(shape))])
    return loudness


def centred(key, dims, deviation, bound, pieces=(), held_as=jnp.bfloat16):
    drawn = deviation * jax.random.normal(key, dims, jnp.float32)
    if pieces:
        drawn = drawn * block_scale(key, dims, pieces, -0.22, 0.18)
    return jnp.clip(drawn, -bound, bound).astype(held_as)


def setup_inputs(seed: int = 0) -> dict:
    key_list = jax.random.split(jax.random.key(seed), 6)
    zonal_wind = centred(key_list[0], (LEV, NLAT, NLON), 1.0, 6.0, ((1, 4), (2, 8)), jnp.float32)
    meridional_wind = centred(key_list[1], (LEV, NLAT, NLON), 1.0, 6.0, ((1, 4), (2, 8)), jnp.float32)
    theta_field = centred(key_list[2], (LEV, NLAT, NLON), 1.0, 6.0, ((1, 4), (2, 8)), jnp.float32)
    pressure = draw_pressure(jax.random.fold_in(key_list[5], 71), 0)
    stiffness = jnp.clip(jnp.exp(math.log(8.0) - 2.0794415 * jax.random.uniform(key_list[4], (LEV, NLAT, NLON), jnp.float32) ** block_scale(key_list[4], (LEV, NLAT, NLON), ((1, 4), (2, 8)), -0.2, 0.2)), 1.0, 8.0)
    return dict(zonal_wind=zonal_wind, meridional_wind=meridional_wind, theta_field=theta_field, pressure=pressure, stiffness=stiffness)


divergence_weight = 0.5
thermal_weight = 0.3
vertical_coupling = 0.5
gradient_weight = 0.5
adjust_weight = 0.5


def extend_global(grid_field, sign_value, margin):
    antipodal = jnp.roll(grid_field, NLON // 2, axis=2)
    south_rows = sign_value * antipodal[:, :margin, :][:, ::-1, :]
    north_rows = sign_value * antipodal[:, -margin:, :][:, ::-1, :]
    tall = jnp.concatenate([south_rows, grid_field, north_rows], axis=1)
    return jnp.concatenate([tall[:, :, -margin:], tall, tall[:, :, :margin]], axis=2)


def make_source(zonal_ext, meridional_ext, pressure, theta_field):
    divergence = 0.5 * (zonal_ext[:, 1:-1, 2:] - zonal_ext[:, 1:-1, :-2]) + 0.5 * (meridional_ext[:, 2:, 1:-1] - meridional_ext[:, :-2, 1:-1])
    return pressure - divergence_weight * divergence + thermal_weight * theta_field


def jacobi(iterate, stiff_ext, source_core):
    levels = iterate.shape[0]
    level_index = jnp.arange(levels)
    vertical = vertical_coupling * ((level_index > 0).astype(jnp.float32) + (level_index < levels - 1).astype(jnp.float32))
    vertical = vertical[:, None, None]
    center = stiff_ext[:, 1:-1, 1:-1]
    east_face = 0.5 * (center + stiff_ext[:, 1:-1, 2:])
    west_face = 0.5 * (center + stiff_ext[:, 1:-1, :-2])
    north_face = 0.5 * (center + stiff_ext[:, 2:, 1:-1])
    south_face = 0.5 * (center + stiff_ext[:, :-2, 1:-1])
    center_value = iterate[:, 1:-1, 1:-1]
    above_level = jnp.concatenate([center_value[1:], jnp.zeros_like(center_value[:1])], axis=0)
    below_level = jnp.concatenate([jnp.zeros_like(center_value[:1]), center_value[:-1]], axis=0)
    numerator = source_core + east_face * iterate[:, 1:-1, 2:] + west_face * iterate[:, 1:-1, :-2]
    numerator = numerator + north_face * iterate[:, 2:, 1:-1] + south_face * iterate[:, :-2, 1:-1]
    numerator = numerator + vertical_coupling * (above_level + below_level)
    denominator = 1.0 + east_face + west_face + north_face + south_face + vertical
    return numerator / denominator


def reference(zonal_wind, meridional_wind, theta_field, pressure, stiffness):
    zonal_ext = extend_global(zonal_wind, -1.0, 1)
    meridional_ext = extend_global(meridional_wind, -1.0, 1)
    source = make_source(zonal_ext, meridional_ext, pressure, theta_field)
    stiff_ext = extend_global(stiffness, 1.0, 1)
    iterate = source
    for sweep_index in range(SWEEPS):
        iterate = jacobi(extend_global(iterate, 1.0, 1), stiff_ext, source)
    final_ext = extend_global(iterate, 1.0, 1)
    east_west = 0.5 * (final_ext[:, 1:-1, 2:] - final_ext[:, 1:-1, :-2])
    north_south = 0.5 * (final_ext[:, 2:, 1:-1] - final_ext[:, :-2, 1:-1])
    zonal_next = zonal_wind - gradient_weight * east_west
    meridional_next = meridional_wind - gradient_weight * north_south
    theta_next = theta_field - adjust_weight * (iterate - pressure)
    return (zonal_next, meridional_next, theta_next, iterate)
```

```python
import functools

import jax
import jax.numpy as jnp
from jax import lax
from jax.experimental import pallas as pl
from jax.experimental.pallas import tpu as pltpu
from jax.sharding import PartitionSpec as P

SWEEPS = 3
HALO = SWEEPS + 1
LANES = 128
EDGE = 8 * HALO
MESH = pl.DeviceIdType.MESH

divergence_weight = 0.5
thermal_weight = 0.3
vertical_coupling = 0.5
gradient_weight = 0.5
adjust_weight = 0.5


def lane_of(rows):
    return lax.broadcasted_iota(jnp.int32, (rows, LANES), 1)


def turn(x, shift, axis=1):
    shift = shift % x.shape[axis]
    return x if shift == 0 else pltpu.roll(x, shift, axis)


def halo_kernel(
    nlon, nlat, u_ref, v_ref, t_ref, p_ref, k_ref,
    ns_ref, ew_ref, cn_ref, own_ref, ns_send, send_sem, recv_sem,
):
    levels, rows, _ = u_ref.shape
    lon, lat = lax.axis_index("lon"), lax.axis_index("lat")
    poles = (lat == 0, lat == nlat - 1)

    def partner(side, shift):
        pole = poles[side]
        row = jnp.where(pole, lat, lat + (1 if side else -1))
        col = lax.rem(lon + shift + nlon + jnp.where(pole, nlon // 2, 0), nlon)
        return {"lon": col, "lat": row}

    def beside(shift):
        return {"lon": lax.rem(lon + shift + nlon, nlon), "lat": lat}

    everyone = [beside(-1), beside(1)]
    everyone += [partner(side, shift) for side in (0, 1) for shift in (-1, 0, 1)]
    barrier = pltpu.get_barrier_semaphore()
    for device in everyone:
        pl.semaphore_signal(barrier, inc=1, device_id=device, device_id_type=MESH)

    lane = lane_of(rows)
    group = lane // HALO
    row_id = lax.broadcasted_iota(jnp.int32, (rows, LANES), 0)
    place = [[jnp.where(poles[s], HALO - 1 - r, r) for r in range(HALO)] for s in (0, 1)]
    first = (0, rows - HALO)
    signs = [jnp.where(poles[s], -1.0, 1.0).astype(jnp.float32) for s in (0, 1)]
    west = jnp.zeros((rows, LANES), jnp.float32)
    east = jnp.zeros((rows, LANES), jnp.float32)
    for level in range(levels):
        u, v, k = u_ref[level], v_ref[level], k_ref[level]
        u_diff = jnp.where(lane == LANES - 1, 0.0, turn(u, -1)) - jnp.where(lane == 0, 0.0, turn(u, 1))
        v_diff = jnp.where(row_id == rows - 1, 0.0, turn(v, -1, 0)) - jnp.where(row_id == 0, 0.0, turn(v, 1, 0))
        part = p_ref[level] - 0.5 * divergence_weight * (u_diff + v_diff) + thermal_weight * t_ref[level]
        for index, field in enumerate((part, k, u, v)):
            slot = index * levels + level
            moved = turn(field, (slot + 1) * HALO)
            east = jnp.where(group == slot, moved, east)
            west = jnp.where(group == (slot + 1) % (LANES // HALO), moved, west)
        for s in (0, 1):
            for r in range(HALO):
                here = slice(first[s] + r, first[s] + r + 1)
                ns_send[s, pl.ds(level * HALO + place[s][r], 1)] = part[here]
                ns_send[s, pl.ds(EDGE + level * HALO + place[s][r], 1)] = k[here]
            edge = slice(0, 1) if s == 0 else slice(rows - 1, rows)
            ns_send[s, 2 * EDGE + level : 2 * EDGE + level + 1] = v[edge] * signs[s]
    west = turn(west, -HALO)
    own_ref[0] = west
    own_ref[1] = east
    base = 2 * EDGE + levels
    for s in (0, 1):
        flip = jnp.where(lane_of(1) >= 3 * EDGE, signs[s], 1.0)
        for r in range(HALO):
            here = slice(first[s] + r, first[s] + r + 1)
            ns_send[s, pl.ds(base + place[s][r], 1)] = west[here] * flip
            ns_send[s, pl.ds(base + HALO + place[s][r], 1)] = east[here] * flip

    pl.semaphore_wait(barrier, len(everyone))
    copies = []

    def send(src, dst, device, out, into):
        copy = pltpu.make_async_remote_copy(
            src_ref=src, dst_ref=dst, send_sem=send_sem.at[out], recv_sem=recv_sem.at[into],
            device_id=device, device_id_type=MESH,
        )
        copy.start()
        copies.append(copy)

    def arrive(dst, into):
        pltpu.make_async_remote_copy(
            src_ref=dst, dst_ref=dst, send_sem=send_sem.at[0], recv_sem=recv_sem.at[into],
            device_id=beside(1), device_id_type=MESH,
        ).wait_recv()

    for s in (0, 1):
        there = jnp.where(poles[s], s, 1 - s)
        send(ns_send.at[s], ns_ref.at[there], partner(s, 0), 2 + s, 2 + there)
        corner = ns_send.at[s, pl.ds(base, 2 * HALO)]
        send(corner, cn_ref.at[there, 1], partner(s, -1), 4 + 2 * s, 4 + 2 * there + 1)
        send(corner, cn_ref.at[there, 0], partner(s, 1), 5 + 2 * s, 4 + 2 * there)
    send(own_ref.at[0], ew_ref.at[1], beside(-1), 0, 1)
    send(own_ref.at[1], ew_ref.at[0], beside(1), 1, 0)
    for side in (0, 1):
        arrive(ew_ref.at[side], side)
        arrive(ns_ref.at[side], 2 + side)
        arrive(cn_ref.at[side, 0], 4 + 2 * side)
        arrive(cn_ref.at[side, 1], 5 + 2 * side)
    for copy in copies:
        copy.wait_send()


def step_kernel(
    u_ref, v_ref, t_ref, p_ref, k_ref, ns_ref, ew_ref, cn_ref, own_ref,
    zonal_ref, meridional_ref, theta_ref, next_ref,
    tall, v_tall, k_tall, source, coef, xa, xb,
):
    levels, rows, _ = u_ref.shape
    high = rows + 2 * HALO
    pad = 8
    core = slice(HALO, HALO + rows)
    base = 2 * EDGE + levels
    top = HALO + rows

    tall[0, core], tall[1, core] = ew_ref[0], own_ref[0]
    tall[2, core], tall[3, core] = own_ref[1], ew_ref[1]
    for s in (0, 1):
        rim = slice(0, HALO) if s == 0 else slice(top, high)
        tall[0, rim] = cn_ref[s, 0, HALO : 2 * HALO]
        tall[1, rim] = ns_ref[s, base : base + HALO]
        tall[2, rim] = ns_ref[s, base + HALO : base + 2 * HALO]
        tall[3, rim] = cn_ref[s, 1, :HALO]

    lane = lane_of(high)
    part, column = lane // EDGE, lane % HALO
    level_id = (lane % EDGE) // HALO
    row_id = lax.broadcasted_iota(jnp.int32, (high, LANES), 0)
    parts = [tall[i] for i in range(4)]

    def side_field(index):
        moved = [turn(parts[i], (i - index) * EDGE) for i in range(4)]
        return jnp.where(part < 2, jnp.where(part == 0, moved[0], moved[1]), jnp.where(part == 2, moved[2], moved[3]))

    def side_east(x):
        return jnp.where(column == HALO - 1, turn(x, HALO - 1 - EDGE), turn(x, -1))

    def side_west(x):
        return jnp.where(column == 0, turn(x, EDGE - HALO + 1), turn(x, 1))

    def fix_rows(partial, v):
        lack_north = (row_id == HALO - 1) | (row_id == top - 1)
        lack_south = (row_id == HALO) | (row_id == top)
        return partial - jnp.where(lack_north, 0.25 * turn(v, -1, 0), 0.0) + jnp.where(lack_south, 0.25 * turn(v, 1, 0), 0.0)

    side_p, side_k, side_u, side_v = [side_field(i) for i in range(4)]
    lack_east = (column == HALO - 1) & (part % 2 == 0)
    lack_west = (column == 0) & (part % 2 == 1)
    side_s = side_p - jnp.where(lack_east, 0.25 * side_east(side_u), 0.0) + jnp.where(lack_west, 0.25 * side_west(side_u), 0.0)
    side_s = fix_rows(side_s, side_v)
    se = 0.5 * (side_k + side_east(side_k))
    sw = 0.5 * (side_k + side_west(side_k))
    sn = 0.5 * (side_k + turn(side_k, -1, 0))
    ss = 0.5 * (side_k + turn(side_k, 1, 0))
    rim_level = (level_id == 0) | (level_id == levels - 1)
    inverse = 1.0 / (1.0 + se + sw + sn + ss + jnp.where(rim_level, vertical_coupling, 2.0 * vertical_coupling))
    se, sw, sn, ss = se * inverse, sw * inverse, sn * inverse, ss * inverse
    s0 = side_s * inverse
    up = jnp.where(level_id == levels - 1, 0.0, vertical_coupling * inverse)
    down = jnp.where(level_id == 0, 0.0, vertical_coupling * inverse)
    side = [side_s]
    for _ in range(SWEEPS):
        x = side[-1]
        side.append(
            s0 + se * side_east(x) + sw * side_west(x) + sn * turn(x, -1, 0) + ss * turn(x, 1, 0)
            + up * turn(x, -HALO) + down * turn(x, HALO)
        )

    def from_west(x, level):
        return turn(x, -(level * HALO + HALO - 1))

    def from_east(x, level):
        return turn(x, LANES - 1 - 3 * EDGE - level * HALO)

    def east_of(x, beyond, level):
        return jnp.where(lane == LANES - 1, from_east(beyond, level), turn(x, -1))

    def west_of(x, beyond, level):
        return jnp.where(lane == 0, from_west(beyond, level), turn(x, 1))

    here = slice(pad, pad + high)
    north, south = slice(pad + 1, pad + 1 + high), slice(pad - 1, pad - 1 + high)
    zero_row = jnp.zeros((1, LANES), jnp.float32)
    lane_core = lane_of(rows)
    for level in range(levels):
        for ref in (xa, xb):
            ref[level, pad - 1 : pad] = zero_row
            ref[level, pad + high : pad + high + 1] = zero_row
        for s, start in ((0, 0), (1, top)):
            source[level, start : start + HALO] = ns_ref[s, level * HALO : (level + 1) * HALO]
            k_tall[level, pad + start : pad + start + HALO] = ns_ref[s, EDGE + level * HALO : EDGE + (level + 1) * HALO]
        k_tall[level, pad - 1 : pad] = zero_row
        k_tall[level, pad + high : pad + high + 1] = zero_row
        k_tall[level, pad + HALO : pad + top] = k_ref[level]
        u, v = u_ref[level], v_ref[level]
        v_tall[HALO - 1 : HALO] = ns_ref[0, 2 * EDGE + level : 2 * EDGE + level + 1]
        v_tall[top : top + 1] = ns_ref[1, 2 * EDGE + level : 2 * EDGE + level + 1]
        v_tall[core] = v
        v_diff = v_tall[HALO + 1 : top + 1] - v_tall[HALO - 1 : top - 1]
        u_diff = jnp.where(lane_core == LANES - 1, 0.0, turn(u, -1)) - jnp.where(lane_core == 0, 0.0, turn(u, 1))
        source[level, core] = p_ref[level] - 0.5 * divergence_weight * (u_diff + v_diff) + thermal_weight * t_ref[level]
        source[level, HALO - 1 : HALO] = source[level, HALO - 1 : HALO] - 0.25 * v[:1]
        source[level, top : top + 1] = source[level, top : top + 1] + 0.25 * v[rows - 1 :]
        full = (
            source[level]
            + jnp.where(lane == 0, 0.25 * from_west(side_u, level), 0.0)
            - jnp.where(lane == LANES - 1, 0.25 * from_east(side_u, level), 0.0)
        )
        k = k_tall[level, here]
        ke = 0.5 * (k + east_of(k, side_k, level))
        kw = 0.5 * (k + west_of(k, side_k, level))
        kn = 0.5 * (k + k_tall[level, north])
        ks = 0.5 * (k + k_tall[level, south])
        count = vertical_coupling * ((level > 0) + (level < levels - 1))
        inv = 1.0 / (1.0 + ke + kw + kn + ks + count)
        xa[level, here] = full
        for index, value in enumerate((full * inv, ke * inv, kw * inv, kn * inv, ks * inv, vertical_coupling * inv)):
            coef[index, level] = value

    now, later = xa, xb
    for sweep in range(SWEEPS):
        beyond = side[sweep]
        for level in range(levels):
            x = now[level, here]
            if level == 0:
                column_sum = now[1, here]
            elif level == levels - 1:
                column_sum = now[level - 1, here]
            else:
                column_sum = now[level + 1, here] + now[level - 1, here]
            later[level, here] = (
                coef[0, level]
                + coef[1, level] * east_of(x, beyond, level)
                + coef[2, level] * west_of(x, beyond, level)
                + coef[3, level] * now[level, north]
                + coef[4, level] * now[level, south]
                + coef[5, level] * column_sum
            )
        now, later = later, now

    lane = lane_core
    beyond = side[SWEEPS][core]
    own = pad + HALO
    for level in range(levels):
        x = now[level, own : own + rows]
        next_ref[level] = x
        zonal_ref[level] = u_ref[level] - 0.5 * gradient_weight * (east_of(x, beyond, level) - west_of(x, beyond, level))
        north_south = now[level, own + 1 : own + 1 + rows] - now[level, own - 1 : own - 1 + rows]
        meridional_ref[level] = v_ref[level] - 0.5 * gradient_weight * north_south
        theta_ref[level] = t_ref[level] - adjust_weight * (x - p_ref[level])


def on_device(nlon, nlat, *fields):
    levels, rows, columns = fields[0].shape
    assert (levels, columns) == (8, LANES)
    f32 = jnp.float32
    vmem = pl.BlockSpec(memory_space=pltpu.VMEM)
    length = 2 * EDGE + levels + 2 * HALO
    high = rows + 2 * HALO
    shapes = [(2, length, LANES), (2, rows, LANES), (2, 2, 2 * HALO, LANES), (2, rows, LANES)]
    halos = pl.pallas_call(
        functools.partial(halo_kernel, nlon, nlat),
        out_shape=[jax.ShapeDtypeStruct(s, f32) for s in shapes],
        in_specs=[vmem] * 5,
        out_specs=[vmem] * 4,
        scratch_shapes=[
            pltpu.VMEM((2, length, LANES), f32),
            pltpu.SemaphoreType.DMA((8,)),
            pltpu.SemaphoreType.DMA((8,)),
        ],
        compiler_params=pltpu.CompilerParams(collective_id=0, has_side_effects=True),
        name="halo",
    )(*fields)
    outputs = pl.pallas_call(
        step_kernel,
        out_shape=[jax.ShapeDtypeStruct((levels, rows, LANES), f32)] * 4,
        in_specs=[vmem] * 9,
        out_specs=[vmem] * 4,
        scratch_shapes=[
            pltpu.VMEM((4, high, LANES), f32),
            pltpu.VMEM((high, LANES), f32),
            pltpu.VMEM((levels, high + 16, LANES), f32),
            pltpu.VMEM((levels, high, LANES), f32),
            pltpu.VMEM((6, levels, high, LANES), f32),
            pltpu.VMEM((levels, high + 16, LANES), f32),
            pltpu.VMEM((levels, high + 16, LANES), f32),
        ],
        name="step",
    )(*fields, *halos)
    return tuple(outputs)


def solution(mesh):
    spec = P(None, "lat", "lon")
    return jax.shard_map(
        functools.partial(on_device, mesh.shape["lon"], mesh.shape["lat"]),
        mesh=mesh,
        in_specs=(spec,) * 5,
        out_specs=(spec,) * 4,
        check_vma=False,
    )
```

```python
import functools

import jax
import jax.numpy as jnp
from jax import lax
from jax.experimental import pallas as pl
from jax.experimental.pallas import tpu as pltpu
from jax.sharding import PartitionSpec as P

SWEEPS = 3
HALO = SWEEPS + 1
CHUNK = 2
LANES = 128
PAD = 8
EDGE = 8 * HALO
MESH = pl.DeviceIdType.MESH

divergence_weight = 0.5
thermal_weight = 0.3
vertical_coupling = 0.5
gradient_weight = 0.5
adjust_weight = 0.5


def lane_of(rows):
    return lax.broadcasted_iota(jnp.int32, (rows, LANES), 1)


def turn(x, shift, axis=1):
    shift = shift % x.shape[axis]
    return x if shift == 0 else pltpu.roll(x, shift, axis)


def kernel(
    nlon, nlat, u_hbm, v_hbm, t_hbm, p_hbm, k_hbm,
    xb, side_ref, u_ref, v_tall, t_ref, p_ref,
    k_tall, ns_ref, ew_ref, cn_ref, own_ref, ns_send,
    tall, source, coef, xa, load_sem, send_sem, recv_sem,
):
    levels, rows, _ = t_ref.shape
    lon, lat = lax.axis_index("lon"), lax.axis_index("lat")
    poles = (lat == 0, lat == nlat - 1)

    def partner(side, shift):
        pole = poles[side]
        row = jnp.where(pole, lat, lat + (1 if side else -1))
        col = lax.rem(lon + shift + nlon + jnp.where(pole, nlon // 2, 0), nlon)
        return {"lon": col, "lat": row}

    def beside(shift):
        return {"lon": lax.rem(lon + shift + nlon, nlon), "lat": lat}

    everyone = [beside(-1), beside(1)]
    everyone += [partner(side, shift) for side in (0, 1) for shift in (-1, 0, 1)]
    barrier = pltpu.get_barrier_semaphore()
    for device in everyone:
        pl.semaphore_signal(barrier, inc=1, device_id=device, device_id_type=MESH)

    loads = [
        pltpu.make_async_copy(src, dst, load_sem.at[i])
        for i, (src, dst) in enumerate((
            (u_hbm, u_ref), (v_hbm, v_tall.at[:, pl.ds(PAD, rows)]), (t_hbm, t_ref),
            (p_hbm, p_ref), (k_hbm, k_tall.at[:, pl.ds(PAD, rows)]),
        ))
    ]
    for load in loads:
        load.start()
    for load in loads:
        load.wait()
    inner = slice(PAD, PAD + rows)
    lane = lane_of(rows)
    group = lane // HALO
    row_id = lax.broadcasted_iota(jnp.int32, (rows, LANES), 0)
    place = [[jnp.where(poles[s], HALO - 1 - r, r) for r in range(HALO)] for s in (0, 1)]
    first = (0, rows - HALO)
    signs = [jnp.where(poles[s], -1.0, 1.0).astype(jnp.float32) for s in (0, 1)]
    west = jnp.zeros((rows, LANES), jnp.float32)
    east = jnp.zeros((rows, LANES), jnp.float32)
    for level in range(levels):
        u, v, k = u_ref[level], v_tall[level, inner], k_tall[level, inner]
        u_diff = jnp.where(lane == LANES - 1, 0.0, turn(u, -1)) - jnp.where(lane == 0, 0.0, turn(u, 1))
        v_diff = jnp.where(row_id == rows - 1, 0.0, turn(v, -1, 0)) - jnp.where(row_id == 0, 0.0, turn(v, 1, 0))
        part = p_ref[level] - 0.5 * divergence_weight * (u_diff + v_diff) + thermal_weight * t_ref[level]
        source[level, inner] = part
        for index, field in enumerate((part, k, u, v)):
            slot = index * levels + level
            moved = turn(field, (slot + 1) * HALO)
            east = jnp.where(group == slot, moved, east)
            west = jnp.where(group == (slot + 1) % (LANES // HALO), moved, west)
        for s in (0, 1):
            for r in range(HALO):
                here = slice(first[s] + r, first[s] + r + 1)
                ns_send[s, pl.ds(level * HALO + place[s][r], 1)] = part[here]
                ns_send[s, pl.ds(EDGE + level * HALO + place[s][r], 1)] = k[here]
            edge = slice(0, 1) if s == 0 else slice(rows - 1, rows)
            ns_send[s, 2 * EDGE + level : 2 * EDGE + level + 1] = v[edge] * signs[s]
    west = turn(west, -HALO)
    own_ref[0] = west
    own_ref[1] = east
    base = 2 * EDGE + levels
    for s in (0, 1):
        flip = jnp.where(lane_of(1) >= 3 * EDGE, signs[s], 1.0)
        for r in range(HALO):
            here = slice(first[s] + r, first[s] + r + 1)
            ns_send[s, pl.ds(base + place[s][r], 1)] = west[here] * flip
            ns_send[s, pl.ds(base + HALO + place[s][r], 1)] = east[here] * flip

    pl.semaphore_wait(barrier, len(everyone))
    copies = []

    def send(src, dst, device, out, into):
        copy = pltpu.make_async_remote_copy(
            src_ref=src, dst_ref=dst, send_sem=send_sem.at[out], recv_sem=recv_sem.at[into],
            device_id=device, device_id_type=MESH,
        )
        copy.start()
        copies.append(copy)

    def arrive(dst, into):
        pltpu.make_async_remote_copy(
            src_ref=dst, dst_ref=dst, send_sem=send_sem.at[0], recv_sem=recv_sem.at[into],
            device_id=beside(1), device_id_type=MESH,
        ).wait_recv()

    for s in (0, 1):
        there = jnp.where(poles[s], s, 1 - s)
        send(ns_send.at[s], ns_ref.at[there], partner(s, 0), 2 + s, 2 + there)
        corner = ns_send.at[s, pl.ds(base, 2 * HALO)]
        send(corner, cn_ref.at[there, 1], partner(s, -1), 4 + 2 * s, 4 + 2 * there + 1)
        send(corner, cn_ref.at[there, 0], partner(s, 1), 5 + 2 * s, 4 + 2 * there)
    send(own_ref.at[0], ew_ref.at[1], beside(-1), 0, 1)
    send(own_ref.at[1], ew_ref.at[0], beside(1), 1, 0)
    for side in (0, 1):
        arrive(ew_ref.at[side], side)
        arrive(ns_ref.at[side], 2 + side)
        arrive(cn_ref.at[side, 0], 4 + 2 * side)
        arrive(cn_ref.at[side, 1], 5 + 2 * side)

    high = rows + 2 * HALO
    core = slice(HALO, HALO + rows)
    top = HALO + rows
    bottom = PAD - HALO

    tall[0, core], tall[1, core] = ew_ref[0], own_ref[0]
    tall[2, core], tall[3, core] = own_ref[1], ew_ref[1]
    for s in (0, 1):
        rim = slice(0, HALO) if s == 0 else slice(top, high)
        tall[0, rim] = cn_ref[s, 0, HALO : 2 * HALO]
        tall[1, rim] = ns_ref[s, base : base + HALO]
        tall[2, rim] = ns_ref[s, base + HALO : base + 2 * HALO]
        tall[3, rim] = cn_ref[s, 1, :HALO]

    lane = lane_of(high)
    part, column = lane // EDGE, lane % HALO
    level_id = (lane % EDGE) // HALO
    row_id = lax.broadcasted_iota(jnp.int32, (high, LANES), 0)
    parts = [tall[i] for i in range(4)]

    def side_field(index):
        moved = [turn(parts[i], (i - index) * EDGE) for i in range(4)]
        return jnp.where(part < 2, jnp.where(part == 0, moved[0], moved[1]), jnp.where(part == 2, moved[2], moved[3]))

    def side_east(x):
        return jnp.where(column == HALO - 1, turn(x, HALO - 1 - EDGE), turn(x, -1))

    def side_west(x):
        return jnp.where(column == 0, turn(x, EDGE - HALO + 1), turn(x, 1))

    def fix_rows(partial, v):
        lack_north = (row_id == HALO - 1) | (row_id == top - 1)
        lack_south = (row_id == HALO) | (row_id == top)
        return partial - jnp.where(lack_north, 0.25 * turn(v, -1, 0), 0.0) + jnp.where(lack_south, 0.25 * turn(v, 1, 0), 0.0)

    side_p, side_k, side_u, side_v = [side_field(i) for i in range(4)]
    lack_east = (column == HALO - 1) & (part % 2 == 0)
    lack_west = (column == 0) & (part % 2 == 1)
    side_s = side_p - jnp.where(lack_east, 0.25 * side_east(side_u), 0.0) + jnp.where(lack_west, 0.25 * side_west(side_u), 0.0)
    side_s = fix_rows(side_s, side_v)
    se = 0.5 * (side_k + side_east(side_k))
    sw = 0.5 * (side_k + side_west(side_k))
    sn = 0.5 * (side_k + turn(side_k, -1, 0))
    ss = 0.5 * (side_k + turn(side_k, 1, 0))
    rim_level = (level_id == 0) | (level_id == levels - 1)
    inverse = 1.0 / (1.0 + se + sw + sn + ss + jnp.where(rim_level, vertical_coupling, 2.0 * vertical_coupling))
    se, sw, sn, ss = se * inverse, sw * inverse, sn * inverse, ss * inverse
    s0 = side_s * inverse
    up = jnp.where(level_id == levels - 1, 0.0, vertical_coupling * inverse)
    down = jnp.where(level_id == 0, 0.0, vertical_coupling * inverse)
    side = [side_s]
    for _ in range(SWEEPS):
        x = side[-1]
        side.append(
            s0 + se * side_east(x) + sw * side_west(x) + sn * turn(x, -1, 0) + ss * turn(x, 1, 0)
            + up * turn(x, -HALO) + down * turn(x, HALO)
        )

    def from_west(x, level):
        return turn(x, -(level * HALO + HALO - 1))

    def from_east(x, level):
        return turn(x, LANES - 1 - 3 * EDGE - level * HALO)

    def east_of(x, beyond, level):
        return jnp.where(lane == LANES - 1, from_east(beyond, level), turn(x, -1))

    def west_of(x, beyond, level):
        return jnp.where(lane == 0, from_west(beyond, level), turn(x, 1))

    here = slice(bottom, bottom + high)
    north, south = slice(bottom + 1, bottom + 1 + high), slice(bottom - 1, bottom - 1 + high)
    zero_row = jnp.zeros((1, LANES), jnp.float32)
    for level in range(levels):
        for ref in (xa, xb, k_tall):
            ref[level, bottom - 1 : bottom] = zero_row
            ref[level, bottom + high : bottom + high + 1] = zero_row
        for s, start in ((0, bottom), (1, PAD + rows)):
            source[level, start : start + HALO] = ns_ref[s, level * HALO : (level + 1) * HALO]
            k_tall[level, start : start + HALO] = ns_ref[s, EDGE + level * HALO : EDGE + (level + 1) * HALO]
        for s, (outer, inside) in enumerate(((PAD - 1, PAD), (PAD + rows, PAD + rows - 1))):
            sign = 0.25 if s == 0 else -0.25
            beyond_v = ns_ref[s, 2 * EDGE + level : 2 * EDGE + level + 1]
            source[level, outer : outer + 1] = source[level, outer : outer + 1] - sign * v_tall[level, inside : inside + 1]
            source[level, inside : inside + 1] = source[level, inside : inside + 1] + sign * beyond_v
        full = (
            source[level, here]
            + jnp.where(lane == 0, 0.25 * from_west(side_u, level), 0.0)
            - jnp.where(lane == LANES - 1, 0.25 * from_east(side_u, level), 0.0)
        )
        k = k_tall[level, here]
        ke = 0.5 * (k + east_of(k, side_k, level))
        kw = 0.5 * (k + west_of(k, side_k, level))
        kn = 0.5 * (k + k_tall[level, north])
        ks = 0.5 * (k + k_tall[level, south])
        count = vertical_coupling * ((level > 0) + (level < levels - 1))
        inv = 1.0 / (1.0 + ke + kw + kn + ks + count)
        xa[level, here] = full
        for index, value in enumerate((full * inv, ke * inv, kw * inv, kn * inv, ks * inv, vertical_coupling * inv)):
            coef[index, level] = value

    now, later = xa, xb
    for sweep in range(SWEEPS):
        beyond = side[sweep]
        for level in range(levels):
            x = now[level, here]
            if level == 0:
                column_sum = now[1, here]
            elif level == levels - 1:
                column_sum = now[level - 1, here]
            else:
                column_sum = now[level + 1, here] + now[level - 1, here]
            later[level, here] = (
                coef[0, level]
                + coef[1, level] * east_of(x, beyond, level)
                + coef[2, level] * west_of(x, beyond, level)
                + coef[3, level] * now[level, north]
                + coef[4, level] * now[level, south]
                + coef[5, level] * column_sum
            )
        now, later = later, now

    side_ref[...] = side[SWEEPS][core]
    for copy in copies:
        copy.wait_send()


def east_west_of(x, beyond, level, lane):
    east = jnp.where(lane == LANES - 1, turn(beyond, LANES - 1 - 3 * EDGE - level * HALO), turn(x, -1))
    west = jnp.where(lane == 0, turn(beyond, -(level * HALO + HALO - 1)), turn(x, 1))
    return east, west


def finish_kernel(
    x_ref, side_ref, u_ref, v_tall, t_ref, p_ref,
    zonal_hbm, meridional_hbm, theta_hbm, next_hbm, out, sem,
):
    levels, rows, _ = u_ref.shape
    lane = lane_of(rows)
    beyond = side_ref[...]
    stores = []
    for level in range(levels):
        x = x_ref[level, PAD : PAD + rows]
        east, west = east_west_of(x, beyond, level, lane)
        north_south = x_ref[level, PAD + 1 : PAD + 1 + rows] - x_ref[level, PAD - 1 : PAD - 1 + rows]
        out[0, level] = u_ref[level] - 0.5 * gradient_weight * (east - west)
        out[1, level] = v_tall[level, PAD : PAD + rows] - 0.5 * gradient_weight * north_south
        out[2, level] = t_ref[level] - adjust_weight * (x - p_ref[level])
        out[3, level] = x
        if (level + 1) % CHUNK == 0:
            done = pl.ds(level + 1 - CHUNK, CHUNK)
            for i, hbm in enumerate((zonal_hbm, meridional_hbm, theta_hbm, next_hbm)):
                store = pltpu.make_async_copy(out.at[i, done], hbm.at[done], sem.at[i, level // CHUNK])
                store.start()
                stores.append(store)
    for store in stores:
        store.wait()


def on_device(nlon, nlat, *fields):
    levels, rows, columns = fields[0].shape
    assert (levels, columns) == (8, LANES)
    f32 = jnp.float32
    length = 2 * EDGE + levels + 2 * HALO
    high = rows + 2 * HALO
    block, padded = (levels, rows, LANES), (levels, rows + 2 * PAD, LANES)
    kept = [padded, (rows, LANES), block, padded, block, block]
    shapes = [
        padded, (2, length, LANES), (2, rows, LANES), (2, 2, 2 * HALO, LANES), (2, rows, LANES), (2, length, LANES),
        (4, high, LANES), padded, (6, levels, high, LANES), padded,
    ]
    held = pl.pallas_call(
        functools.partial(kernel, nlon, nlat),
        out_shape=[pltpu.VMEM(shape, f32) for shape in kept],
        in_specs=[pl.BlockSpec(memory_space=pl.ANY)] * 5,
        out_specs=[pl.BlockSpec(memory_space=pltpu.VMEM)] * 6,
        scratch_shapes=[pltpu.VMEM(shape, f32) for shape in shapes]
        + [pltpu.SemaphoreType.DMA((5,)), pltpu.SemaphoreType.DMA((8,)), pltpu.SemaphoreType.DMA((8,))],
        compiler_params=pltpu.CompilerParams(collective_id=0, has_side_effects=True),
        name="halo_step",
    )(*fields)
    held = [pltpu.with_memory_space_constraint(x, pltpu.VMEM) for x in held]
    outputs = pl.pallas_call(
        finish_kernel,
        out_shape=[jax.ShapeDtypeStruct(block, f32)] * 4,
        in_specs=[pl.BlockSpec(memory_space=pltpu.VMEM)] * 6,
        out_specs=[pl.BlockSpec(memory_space=pl.ANY)] * 4,
        scratch_shapes=[
            pltpu.VMEM((4, levels, rows, LANES), f32),
            pltpu.SemaphoreType.DMA((4, levels // CHUNK)),
        ],
        name="finish",
    )(*held)
    return tuple(outputs)


def solution(mesh):
    spec = P(None, "lat", "lon")
    return jax.shard_map(
        functools.partial(on_device, mesh.shape["lon"], mesh.shape["lat"]),
        mesh=mesh,
        in_specs=(spec,) * 5,
        out_specs=(spec,) * 4,
        check_vma=False,
    )
```

```python
import functools

import jax
import jax.numpy as jnp
from jax import lax
from jax.experimental import pallas as pl
from jax.experimental.pallas import tpu as pltpu
from jax.sharding import PartitionSpec as P

SWEEPS = 3
HALO = SWEEPS + 1
CHUNK = 4
LANES = 128
PAD = 8
EDGE = 8 * HALO
MESH = pl.DeviceIdType.MESH

divergence_weight = 0.5
thermal_weight = 0.3
vertical_coupling = 0.5
gradient_weight = 0.5
adjust_weight = 0.5


def lane_of(rows):
    return lax.broadcasted_iota(jnp.int32, (rows, LANES), 1)


def turn(x, shift, axis=1):
    shift = shift % x.shape[axis]
    return x if shift == 0 else pltpu.roll(x, shift, axis)


def kernel(
    nlon, nlat, u_hbm, v_hbm, t_hbm, p_hbm, k_hbm,
    xb, side_ref, u_ref, v_tall, t_ref, p_ref,
    k_tall, ns_ref, ew_ref, cn_ref, own_ref, ns_send,
    tall, coef, xa, load_sem, send_sem, recv_sem,
):
    levels, rows, _ = t_ref.shape
    lon, lat = lax.axis_index("lon"), lax.axis_index("lat")
    poles = (lat == 0, lat == nlat - 1)

    def partner(side, shift):
        pole = poles[side]
        row = jnp.where(pole, lat, lat + (1 if side else -1))
        col = lax.rem(lon + shift + nlon + jnp.where(pole, nlon // 2, 0), nlon)
        return {"lon": col, "lat": row}

    def beside(shift):
        return {"lon": lax.rem(lon + shift + nlon, nlon), "lat": lat}

    everyone = [beside(-1), beside(1)]
    everyone += [partner(side, shift) for side in (0, 1) for shift in (-1, 0, 1)]
    barrier = pltpu.get_barrier_semaphore()
    for device in everyone:
        pl.semaphore_signal(barrier, inc=1, device_id=device, device_id_type=MESH)

    loads = [
        pltpu.make_async_copy(src, dst, load_sem.at[i])
        for i, (src, dst) in enumerate((
            (u_hbm, u_ref), (v_hbm, v_tall.at[:, pl.ds(PAD, rows)]), (t_hbm, t_ref),
            (p_hbm, p_ref), (k_hbm, k_tall.at[:, pl.ds(PAD, rows)]),
        ))
    ]
    for load in loads:
        load.start()
    for load in loads:
        load.wait()
    inner = slice(PAD, PAD + rows)
    lane = lane_of(rows)
    group = lane // HALO
    row_id = lax.broadcasted_iota(jnp.int32, (rows, LANES), 0)
    place = [[jnp.where(poles[s], HALO - 1 - r, r) for r in range(HALO)] for s in (0, 1)]
    first = (0, rows - HALO)
    signs = [jnp.where(poles[s], -1.0, 1.0).astype(jnp.float32) for s in (0, 1)]
    west = jnp.zeros((rows, LANES), jnp.float32)
    east = jnp.zeros((rows, LANES), jnp.float32)
    for level in range(levels):
        u, v, k = u_ref[level], v_tall[level, inner], k_tall[level, inner]
        u_diff = jnp.where(lane == LANES - 1, 0.0, turn(u, -1)) - jnp.where(lane == 0, 0.0, turn(u, 1))
        v_diff = jnp.where(row_id == rows - 1, 0.0, turn(v, -1, 0)) - jnp.where(row_id == 0, 0.0, turn(v, 1, 0))
        part = p_ref[level] - 0.5 * divergence_weight * (u_diff + v_diff) + thermal_weight * t_ref[level]
        xa[level, inner] = part
        for index, field in enumerate((part, k, u, v)):
            slot = index * levels + level
            moved = turn(field, (slot + 1) * HALO)
            east = jnp.where(group == slot, moved, east)
            west = jnp.where(group == (slot + 1) % (LANES // HALO), moved, west)
    west = turn(west, -HALO)
    own_ref[0] = west
    own_ref[1] = east
    base = 2 * EDGE + levels
    for s in (0, 1):
        flip = jnp.where(lane_of(1) >= 3 * EDGE, signs[s], 1.0)
        for r in range(HALO):
            here = slice(first[s] + r, first[s] + r + 1)
            ns_send[s, pl.ds(base + place[s][r], 1)] = west[here] * flip
            ns_send[s, pl.ds(base + HALO + place[s][r], 1)] = east[here] * flip

    pl.semaphore_wait(barrier, len(everyone))
    copies = []

    def send(src, dst, device, out, into):
        copy = pltpu.make_async_remote_copy(
            src_ref=src, dst_ref=dst, send_sem=send_sem.at[out], recv_sem=recv_sem.at[into],
            device_id=device, device_id_type=MESH,
        )
        copy.start()
        copies.append(copy)

    def arrive(dst, into):
        pltpu.make_async_remote_copy(
            src_ref=dst, dst_ref=dst, send_sem=send_sem.at[0], recv_sem=recv_sem.at[into],
            device_id=beside(1), device_id_type=MESH,
        ).wait_recv()

    send(own_ref.at[0], ew_ref.at[1], beside(-1), 0, 1)
    send(own_ref.at[1], ew_ref.at[0], beside(1), 1, 0)
    there = [jnp.where(poles[s], s, 1 - s) for s in (0, 1)]
    for s in (0, 1):
        corner = ns_send.at[s, pl.ds(base, 2 * HALO)]
        send(corner, cn_ref.at[there[s], 1], partner(s, -1), 4 + 2 * s, 4 + 2 * there[s] + 1)
        send(corner, cn_ref.at[there[s], 0], partner(s, 1), 5 + 2 * s, 4 + 2 * there[s])
    for s in (0, 1):
        for level in range(levels):
            for r in range(HALO):
                here = slice(PAD + first[s] + r, PAD + first[s] + r + 1)
                ns_send[s, pl.ds(level * HALO + place[s][r], 1)] = xa[level, here]
                ns_send[s, pl.ds(EDGE + level * HALO + place[s][r], 1)] = k_tall[level, here]
            edge = PAD if s == 0 else PAD + rows - 1
            ns_send[s, 2 * EDGE + level : 2 * EDGE + level + 1] = v_tall[level, edge : edge + 1] * signs[s]
        send(ns_send.at[s], ns_ref.at[there[s]], partner(s, 0), 2 + s, 2 + there[s])

    high = rows + 2 * HALO
    core = slice(HALO, HALO + rows)
    top = HALO + rows
    bottom = PAD - HALO
    zero_row = jnp.zeros((1, LANES), jnp.float32)

    def weigh(level, start, count):
        at = lambda shift: slice(start + shift, start + shift + count)
        k = k_tall[level, at(0)]
        ke = 0.5 * (k + turn(k, -1))
        kw = 0.5 * (k + turn(k, 1))
        kn = 0.5 * (k + k_tall[level, at(1)])
        ks = 0.5 * (k + k_tall[level, at(-1)])
        vertical = vertical_coupling * ((level > 0) + (level < levels - 1))
        inv = 1.0 / (1.0 + ke + kw + kn + ks + vertical)
        found = (xa[level, at(0)] * inv, ke * inv, kw * inv, kn * inv, ks * inv, vertical_coupling * inv)
        for index, value in enumerate(found):
            coef[index, level, at(0)] = value

    for level in range(levels):
        for ref in (xa, xb, k_tall):
            ref[level, bottom - 1 : bottom] = zero_row
            ref[level, bottom + high : bottom + high + 1] = zero_row
        for start in (bottom, PAD + rows):
            k_tall[level, start : start + HALO] = jnp.zeros((HALO, LANES), jnp.float32)
        weigh(level, PAD, rows)

    for side in (0, 1):
        arrive(ew_ref.at[side], side)
        arrive(ns_ref.at[side], 2 + side)
        arrive(cn_ref.at[side, 0], 4 + 2 * side)
        arrive(cn_ref.at[side, 1], 5 + 2 * side)

    tall[0, core], tall[1, core] = ew_ref[0], own_ref[0]
    tall[2, core], tall[3, core] = own_ref[1], ew_ref[1]
    for s in (0, 1):
        rim = slice(0, HALO) if s == 0 else slice(top, high)
        tall[0, rim] = cn_ref[s, 0, HALO : 2 * HALO]
        tall[1, rim] = ns_ref[s, base : base + HALO]
        tall[2, rim] = ns_ref[s, base + HALO : base + 2 * HALO]
        tall[3, rim] = cn_ref[s, 1, :HALO]

    lane = lane_of(high)
    part, column = lane // EDGE, lane % HALO
    level_id = (lane % EDGE) // HALO
    row_id = lax.broadcasted_iota(jnp.int32, (high, LANES), 0)
    parts = [tall[i] for i in range(4)]

    def side_field(index):
        moved = [turn(parts[i], (i - index) * EDGE) for i in range(4)]
        return jnp.where(part < 2, jnp.where(part == 0, moved[0], moved[1]), jnp.where(part == 2, moved[2], moved[3]))

    def side_east(x):
        return jnp.where(column == HALO - 1, turn(x, HALO - 1 - EDGE), turn(x, -1))

    def side_west(x):
        return jnp.where(column == 0, turn(x, EDGE - HALO + 1), turn(x, 1))

    def fix_rows(partial, v):
        lack_north = (row_id == HALO - 1) | (row_id == top - 1)
        lack_south = (row_id == HALO) | (row_id == top)
        return partial - jnp.where(lack_north, 0.25 * turn(v, -1, 0), 0.0) + jnp.where(lack_south, 0.25 * turn(v, 1, 0), 0.0)

    side_p, side_k, side_u, side_v = [side_field(i) for i in range(4)]
    lack_east = (column == HALO - 1) & (part % 2 == 0)
    lack_west = (column == 0) & (part % 2 == 1)
    side_s = side_p - jnp.where(lack_east, 0.25 * side_east(side_u), 0.0) + jnp.where(lack_west, 0.25 * side_west(side_u), 0.0)
    side_s = fix_rows(side_s, side_v)
    se = 0.5 * (side_k + side_east(side_k))
    sw = 0.5 * (side_k + side_west(side_k))
    sn = 0.5 * (side_k + turn(side_k, -1, 0))
    ss = 0.5 * (side_k + turn(side_k, 1, 0))
    rim_level = (level_id == 0) | (level_id == levels - 1)
    inverse = 1.0 / (1.0 + se + sw + sn + ss + jnp.where(rim_level, vertical_coupling, 2.0 * vertical_coupling))
    se, sw, sn, ss = se * inverse, sw * inverse, sn * inverse, ss * inverse
    s0 = side_s * inverse
    up = jnp.where(level_id == levels - 1, 0.0, vertical_coupling * inverse)
    down = jnp.where(level_id == 0, 0.0, vertical_coupling * inverse)
    side = [side_s]
    for _ in range(SWEEPS):
        x = side[-1]
        side.append(
            s0 + se * side_east(x) + sw * side_west(x) + sn * turn(x, -1, 0) + ss * turn(x, 1, 0)
            + up * turn(x, -HALO) + down * turn(x, HALO)
        )

    rims = [jnp.where(column == HALO - 1, turn(x, -(EDGE + HALO)), x) for x in side]
    edge = (lane == 0) | (lane == LANES - 1)

    def with_edges(x, step, level):
        return jnp.where(edge, turn(rims[step], -(EDGE + level * HALO)), x)

    here = slice(bottom, bottom + high)
    north, south = slice(bottom + 1, bottom + 1 + high), slice(bottom - 1, bottom - 1 + high)
    for level in range(levels):
        for s, start in ((0, bottom), (1, PAD + rows)):
            xa[level, start : start + HALO] = ns_ref[s, level * HALO : (level + 1) * HALO]
            k_tall[level, start : start + HALO] = ns_ref[s, EDGE + level * HALO : EDGE + (level + 1) * HALO]
        for s, (outer, inside) in enumerate(((PAD - 1, PAD), (PAD + rows, PAD + rows - 1))):
            sign = 0.25 if s == 0 else -0.25
            beyond_v = ns_ref[s, 2 * EDGE + level : 2 * EDGE + level + 1]
            xa[level, outer : outer + 1] = xa[level, outer : outer + 1] - sign * v_tall[level, inside : inside + 1]
            xa[level, inside : inside + 1] = xa[level, inside : inside + 1] + sign * beyond_v
        for start in (bottom, PAD + rows - HALO):
            weigh(level, start, 2 * HALO)
        xa[level, here] = with_edges(xa[level, here], 0, level)

    now, later = xa, xb
    for sweep in range(SWEEPS):
        for level in range(levels):
            x = now[level, here]
            if level == 0:
                column_sum = now[1, here]
            elif level == levels - 1:
                column_sum = now[level - 1, here]
            else:
                column_sum = now[level + 1, here] + now[level - 1, here]
            value = (
                coef[0, level, here]
                + coef[1, level, here] * turn(x, -1)
                + coef[2, level, here] * turn(x, 1)
                + coef[3, level, here] * now[level, north]
                + coef[4, level, here] * now[level, south]
                + coef[5, level, here] * column_sum
            )
            later[level, here] = with_edges(value, sweep + 1, level)
        now, later = later, now

    side_ref[...] = side[SWEEPS][core]
    for copy in copies:
        copy.wait_send()


def east_west_of(x, beyond, level, lane):
    east = jnp.where(lane == LANES - 1, turn(beyond, LANES - 1 - 3 * EDGE - level * HALO), turn(x, -1))
    west = jnp.where(lane == 0, turn(beyond, -(level * HALO + HALO - 1)), turn(x, 1))
    return east, west


def finish_kernel(
    x_ref, side_ref, u_ref, v_tall, t_ref, p_ref,
    zonal_hbm, meridional_hbm, theta_hbm, next_hbm, out, sem,
):
    levels, rows, _ = u_ref.shape
    lane = lane_of(rows)
    beyond = side_ref[...]
    stores = [pltpu.make_async_copy(x_ref.at[:, pl.ds(PAD, rows)], next_hbm, sem.at[3, 0])]
    stores[0].start()
    for level in range(levels):
        x = x_ref[level, PAD : PAD + rows]
        east, west = east_west_of(x, beyond, level, lane)
        north_south = x_ref[level, PAD + 1 : PAD + 1 + rows] - x_ref[level, PAD - 1 : PAD - 1 + rows]
        out[0, level] = u_ref[level] - 0.5 * gradient_weight * (east - west)
        out[1, level] = v_tall[level, PAD : PAD + rows] - 0.5 * gradient_weight * north_south
        out[2, level] = t_ref[level] - adjust_weight * (x - p_ref[level])
        if (level + 1) % CHUNK == 0:
            done = pl.ds(level + 1 - CHUNK, CHUNK)
            for i, hbm in enumerate((zonal_hbm, meridional_hbm, theta_hbm)):
                store = pltpu.make_async_copy(out.at[i, done], hbm.at[done], sem.at[i, level // CHUNK])
                store.start()
                stores.append(store)
    for store in stores:
        store.wait()


def on_device(nlon, nlat, *fields):
    levels, rows, columns = fields[0].shape
    assert (levels, columns) == (8, LANES)
    f32 = jnp.float32
    length = 2 * EDGE + levels + 2 * HALO
    high = rows + 2 * HALO
    block, padded = (levels, rows, LANES), (levels, rows + 2 * PAD, LANES)
    kept = [padded, (rows, LANES), block, padded, block, block]
    shapes = [
        padded, (2, length, LANES), (2, rows, LANES), (2, 2, 2 * HALO, LANES), (2, rows, LANES), (2, length, LANES),
        (4, high, LANES), (6, levels, rows + 2 * PAD, LANES), padded,
    ]
    held = pl.pallas_call(
        functools.partial(kernel, nlon, nlat),
        out_shape=[pltpu.VMEM(shape, f32) for shape in kept],
        in_specs=[pl.BlockSpec(memory_space=pl.ANY)] * 5,
        out_specs=[pl.BlockSpec(memory_space=pltpu.VMEM)] * 6,
        scratch_shapes=[pltpu.VMEM(shape, f32) for shape in shapes]
        + [pltpu.SemaphoreType.DMA((5,)), pltpu.SemaphoreType.DMA((8,)), pltpu.SemaphoreType.DMA((8,))],
        compiler_params=pltpu.CompilerParams(collective_id=0, has_side_effects=True),
        name="halo_step",
    )(*fields)
    held = [pltpu.with_memory_space_constraint(x, pltpu.VMEM) for x in held]
    outputs = pl.pallas_call(
        finish_kernel,
        out_shape=[jax.ShapeDtypeStruct(block, f32)] * 4,
        in_specs=[pl.BlockSpec(memory_space=pltpu.VMEM)] * 6,
        out_specs=[pl.BlockSpec(memory_space=pl.ANY)] * 4,
        scratch_shapes=[
            pltpu.VMEM((3, levels, rows, LANES), f32),
            pltpu.SemaphoreType.DMA((4, levels // CHUNK)),
        ],
        name="finish",
    )(*held)
    return tuple(outputs)


def solution(mesh):
    spec = P(None, "lat", "lon")
    return jax.shard_map(
        functools.partial(on_device, mesh.shape["lon"], mesh.shape["lat"]),
        mesh=mesh,
        in_specs=(spec,) * 5,
        out_specs=(spec,) * 4,
        check_vma=False,
    )
```

```python
import functools

import jax
import jax.numpy as jnp
from jax import lax
from jax.experimental import pallas as pl
from jax.experimental.pallas import tpu as pltpu
from jax.sharding import PartitionSpec as P

SWEEPS = 3
HALO = SWEEPS + 1
CHUNK = 4
LANES = 128
PAD = 8
EDGE = 8 * HALO
MESH = pl.DeviceIdType.MESH

divergence_weight = 0.5
thermal_weight = 0.3
vertical_coupling = 0.5
gradient_weight = 0.5
adjust_weight = 0.5


def lane_of(rows):
    return lax.broadcasted_iota(jnp.int32, (rows, LANES), 1)


def turn(x, shift, axis=1):
    shift = shift % x.shape[axis]
    return x if shift == 0 else pltpu.roll(x, shift, axis)


def kernel(
    nlon, nlat, u_hbm, v_hbm, t_hbm, p_hbm, k_hbm,
    xb, side_ref, u_ref, v_tall, t_ref, p_ref,
    k_tall, ns_ref, ew_ref, cn_ref, own_ref, ns_send,
    tall, coef, xa, load_sem, send_sem, recv_sem,
):
    levels, rows, _ = t_ref.shape
    lon, lat = lax.axis_index("lon"), lax.axis_index("lat")
    poles = (lat == 0, lat == nlat - 1)

    def partner(side, shift):
        pole = poles[side]
        row = jnp.where(pole, lat, lat + (1 if side else -1))
        col = lax.rem(lon + shift + nlon + jnp.where(pole, nlon // 2, 0), nlon)
        return {"lon": col, "lat": row}

    def beside(shift):
        return {"lon": lax.rem(lon + shift + nlon, nlon), "lat": lat}

    everyone = [beside(-1), beside(1)]
    everyone += [partner(side, shift) for side in (0, 1) for shift in (-1, 0, 1)]
    barrier = pltpu.get_barrier_semaphore()
    for device in everyone:
        pl.semaphore_signal(barrier, inc=1, device_id=device, device_id_type=MESH)

    loads = [
        pltpu.make_async_copy(src, dst, load_sem.at[i])
        for i, (src, dst) in enumerate((
            (k_hbm, k_tall.at[:, pl.ds(PAD, rows)]), (u_hbm, u_ref),
            (v_hbm, v_tall.at[:, pl.ds(PAD, rows)]), (t_hbm, t_ref), (p_hbm, p_ref),
        ))
    ]
    for load in loads:
        load.start()
    inner = slice(PAD, PAD + rows)
    lane = lane_of(rows)
    group = lane // HALO
    row_id = lax.broadcasted_iota(jnp.int32, (rows, LANES), 0)
    place = [[jnp.where(poles[s], HALO - 1 - r, r) for r in range(HALO)] for s in (0, 1)]
    first = (0, rows - HALO)
    signs = [jnp.where(poles[s], -1.0, 1.0).astype(jnp.float32) for s in (0, 1)]
    west = jnp.zeros((rows, LANES), jnp.float32)
    east = jnp.zeros((rows, LANES), jnp.float32)

    def packed(pair, field, index, level):
        slot = index * levels + level
        moved = turn(field, (slot + 1) * HALO)
        west, east = pair
        return (
            jnp.where(group == (slot + 1) % (LANES // HALO), moved, west),
            jnp.where(group == slot, moved, east),
        )

    pair = (west, east)
    for index, ref, load in ((1, k_tall, loads[0]), (2, u_ref, loads[1]), (3, v_tall, loads[2])):
        load.wait()
        for level in range(levels):
            pair = packed(pair, ref[level] if ref is u_ref else ref[level, inner], index, level)
    loads[3].wait()
    loads[4].wait()
    for level in range(levels):
        u, v = u_ref[level], v_tall[level, inner]
        u_diff = jnp.where(lane == LANES - 1, 0.0, turn(u, -1)) - jnp.where(lane == 0, 0.0, turn(u, 1))
        v_diff = jnp.where(row_id == rows - 1, 0.0, turn(v, -1, 0)) - jnp.where(row_id == 0, 0.0, turn(v, 1, 0))
        part = p_ref[level] - 0.5 * divergence_weight * (u_diff + v_diff) + thermal_weight * t_ref[level]
        xa[level, inner] = part
        pair = packed(pair, part, 0, level)
    west, east = pair
    west = turn(west, -HALO)
    own_ref[0] = west
    own_ref[1] = east
    base = 2 * EDGE + levels
    for s in (0, 1):
        flip = jnp.where(lane_of(1) >= 3 * EDGE, signs[s], 1.0)
        for r in range(HALO):
            here = slice(first[s] + r, first[s] + r + 1)
            ns_send[s, pl.ds(base + place[s][r], 1)] = west[here] * flip
            ns_send[s, pl.ds(base + HALO + place[s][r], 1)] = east[here] * flip

    pl.semaphore_wait(barrier, len(everyone))
    copies = []

    def send(src, dst, device, out, into):
        copy = pltpu.make_async_remote_copy(
            src_ref=src, dst_ref=dst, send_sem=send_sem.at[out], recv_sem=recv_sem.at[into],
            device_id=device, device_id_type=MESH,
        )
        copy.start()
        copies.append(copy)

    def arrive(dst, into):
        pltpu.make_async_remote_copy(
            src_ref=dst, dst_ref=dst, send_sem=send_sem.at[0], recv_sem=recv_sem.at[into],
            device_id=beside(1), device_id_type=MESH,
        ).wait_recv()

    send(own_ref.at[0], ew_ref.at[1], beside(-1), 0, 1)
    send(own_ref.at[1], ew_ref.at[0], beside(1), 1, 0)
    there = [jnp.where(poles[s], s, 1 - s) for s in (0, 1)]
    for s in (0, 1):
        corner = ns_send.at[s, pl.ds(base, 2 * HALO)]
        send(corner, cn_ref.at[there[s], 1], partner(s, -1), 4 + 2 * s, 4 + 2 * there[s] + 1)
        send(corner, cn_ref.at[there[s], 0], partner(s, 1), 5 + 2 * s, 4 + 2 * there[s])
    for s in (0, 1):
        for level in range(levels):
            for r in range(HALO):
                here = slice(PAD + first[s] + r, PAD + first[s] + r + 1)
                ns_send[s, pl.ds(level * HALO + place[s][r], 1)] = xa[level, here]
                ns_send[s, pl.ds(EDGE + level * HALO + place[s][r], 1)] = k_tall[level, here]
            edge = PAD if s == 0 else PAD + rows - 1
            ns_send[s, 2 * EDGE + level : 2 * EDGE + level + 1] = v_tall[level, edge : edge + 1] * signs[s]
        send(ns_send.at[s], ns_ref.at[there[s]], partner(s, 0), 2 + s, 2 + there[s])

    high = rows + 2 * HALO
    core = slice(HALO, HALO + rows)
    top = HALO + rows
    bottom = PAD - HALO
    zero_row = jnp.zeros((1, LANES), jnp.float32)

    def weigh(level, start, count):
        at = lambda shift: slice(start + shift, start + shift + count)
        k = k_tall[level, at(0)]
        ke = 0.5 * (k + turn(k, -1))
        kw = 0.5 * (k + turn(k, 1))
        kn = 0.5 * (k + k_tall[level, at(1)])
        ks = 0.5 * (k + k_tall[level, at(-1)])
        vertical = vertical_coupling * ((level > 0) + (level < levels - 1))
        inv = 1.0 / (1.0 + ke + kw + kn + ks + vertical)
        found = (xa[level, at(0)] * inv, ke * inv, kw * inv, kn * inv, ks * inv, vertical_coupling * inv)
        for index, value in enumerate(found):
            coef[index, level, at(0)] = value

    for level in range(levels):
        for ref in (xa, xb, k_tall):
            ref[level, bottom - 1 : bottom] = zero_row
            ref[level, bottom + high : bottom + high + 1] = zero_row
        for start in (bottom, PAD + rows):
            k_tall[level, start : start + HALO] = jnp.zeros((HALO, LANES), jnp.float32)
        weigh(level, PAD, rows)

    for side in (0, 1):
        arrive(ns_ref.at[side], 2 + side)
    for level in range(levels):
        for s, start in ((0, bottom), (1, PAD + rows)):
            xa[level, start : start + HALO] = ns_ref[s, level * HALO : (level + 1) * HALO]
            k_tall[level, start : start + HALO] = ns_ref[s, EDGE + level * HALO : EDGE + (level + 1) * HALO]
        for s, (outer, inside) in enumerate(((PAD - 1, PAD), (PAD + rows, PAD + rows - 1))):
            sign = 0.25 if s == 0 else -0.25
            beyond_v = ns_ref[s, 2 * EDGE + level : 2 * EDGE + level + 1]
            xa[level, outer : outer + 1] = xa[level, outer : outer + 1] - sign * v_tall[level, inside : inside + 1]
            xa[level, inside : inside + 1] = xa[level, inside : inside + 1] + sign * beyond_v
        for start in (bottom, PAD + rows - HALO):
            weigh(level, start, 2 * HALO)
    for side in (0, 1):
        arrive(ew_ref.at[side], side)
        arrive(cn_ref.at[side, 0], 4 + 2 * side)
        arrive(cn_ref.at[side, 1], 5 + 2 * side)

    tall[0, core], tall[1, core] = ew_ref[0], own_ref[0]
    tall[2, core], tall[3, core] = own_ref[1], ew_ref[1]
    for s in (0, 1):
        rim = slice(0, HALO) if s == 0 else slice(top, high)
        tall[0, rim] = cn_ref[s, 0, HALO : 2 * HALO]
        tall[1, rim] = ns_ref[s, base : base + HALO]
        tall[2, rim] = ns_ref[s, base + HALO : base + 2 * HALO]
        tall[3, rim] = cn_ref[s, 1, :HALO]

    lane = lane_of(high)
    part, column = lane // EDGE, lane % HALO
    level_id = (lane % EDGE) // HALO
    row_id = lax.broadcasted_iota(jnp.int32, (high, LANES), 0)
    parts = [tall[i] for i in range(4)]

    def side_field(index):
        moved = [turn(parts[i], (i - index) * EDGE) for i in range(4)]
        return jnp.where(part < 2, jnp.where(part == 0, moved[0], moved[1]), jnp.where(part == 2, moved[2], moved[3]))

    def side_east(x):
        return jnp.where(column == HALO - 1, turn(x, HALO - 1 - EDGE), turn(x, -1))

    def side_west(x):
        return jnp.where(column == 0, turn(x, EDGE - HALO + 1), turn(x, 1))

    def fix_rows(partial, v):
        lack_north = (row_id == HALO - 1) | (row_id == top - 1)
        lack_south = (row_id == HALO) | (row_id == top)
        return partial - jnp.where(lack_north, 0.25 * turn(v, -1, 0), 0.0) + jnp.where(lack_south, 0.25 * turn(v, 1, 0), 0.0)

    side_p, side_k, side_u, side_v = [side_field(i) for i in range(4)]
    lack_east = (column == HALO - 1) & (part % 2 == 0)
    lack_west = (column == 0) & (part % 2 == 1)
    side_s = side_p - jnp.where(lack_east, 0.25 * side_east(side_u), 0.0) + jnp.where(lack_west, 0.25 * side_west(side_u), 0.0)
    side_s = fix_rows(side_s, side_v)
    se = 0.5 * (side_k + side_east(side_k))
    sw = 0.5 * (side_k + side_west(side_k))
    sn = 0.5 * (side_k + turn(side_k, -1, 0))
    ss = 0.5 * (side_k + turn(side_k, 1, 0))
    rim_level = (level_id == 0) | (level_id == levels - 1)
    inverse = 1.0 / (1.0 + se + sw + sn + ss + jnp.where(rim_level, vertical_coupling, 2.0 * vertical_coupling))
    se, sw, sn, ss = se * inverse, sw * inverse, sn * inverse, ss * inverse
    s0 = side_s * inverse
    up = jnp.where(level_id == levels - 1, 0.0, vertical_coupling * inverse)
    down = jnp.where(level_id == 0, 0.0, vertical_coupling * inverse)
    side = [side_s]
    for _ in range(SWEEPS):
        x = side[-1]
        side.append(
            s0 + se * side_east(x) + sw * side_west(x) + sn * turn(x, -1, 0) + ss * turn(x, 1, 0)
            + up * turn(x, -HALO) + down * turn(x, HALO)
        )

    rims = [jnp.where(column == HALO - 1, turn(x, -(EDGE + HALO)), x) for x in side]
    edge = (lane == 0) | (lane == LANES - 1)

    def with_edges(x, step, level):
        return jnp.where(edge, turn(rims[step], -(EDGE + level * HALO)), x)

    here = slice(bottom, bottom + high)
    north, south = slice(bottom + 1, bottom + 1 + high), slice(bottom - 1, bottom - 1 + high)
    for level in range(levels):
        xa[level, here] = with_edges(xa[level, here], 0, level)

    now, later = xa, xb
    for sweep in range(SWEEPS):
        for level in range(levels):
            x = now[level, here]
            if level == 0:
                column_sum = now[1, here]
            elif level == levels - 1:
                column_sum = now[level - 1, here]
            else:
                column_sum = now[level + 1, here] + now[level - 1, here]
            value = (
                coef[0, level, here]
                + coef[1, level, here] * turn(x, -1)
                + coef[2, level, here] * turn(x, 1)
                + coef[3, level, here] * now[level, north]
                + coef[4, level, here] * now[level, south]
                + coef[5, level, here] * column_sum
            )
            later[level, here] = with_edges(value, sweep + 1, level)
        now, later = later, now

    side_ref[...] = side[SWEEPS][core]
    for copy in copies:
        copy.wait_send()


def east_west_of(x, beyond, level, lane):
    east = jnp.where(lane == LANES - 1, turn(beyond, LANES - 1 - 3 * EDGE - level * HALO), turn(x, -1))
    west = jnp.where(lane == 0, turn(beyond, -(level * HALO + HALO - 1)), turn(x, 1))
    return east, west


def finish_kernel(
    x_ref, side_ref, u_ref, v_tall, t_ref, p_ref,
    zonal_hbm, meridional_hbm, theta_hbm, next_hbm, out, sem,
):
    levels, rows, _ = u_ref.shape
    lane = lane_of(rows)
    beyond = side_ref[...]
    stores = [pltpu.make_async_copy(x_ref.at[:, pl.ds(PAD, rows)], next_hbm, sem.at[3, 0])]
    stores[0].start()
    for level in range(levels):
        x = x_ref[level, PAD : PAD + rows]
        east, west = east_west_of(x, beyond, level, lane)
        north_south = x_ref[level, PAD + 1 : PAD + 1 + rows] - x_ref[level, PAD - 1 : PAD - 1 + rows]
        out[0, level] = u_ref[level] - 0.5 * gradient_weight * (east - west)
        out[1, level] = v_tall[level, PAD : PAD + rows] - 0.5 * gradient_weight * north_south
        out[2, level] = t_ref[level] - adjust_weight * (x - p_ref[level])
        if (level + 1) % CHUNK == 0:
            done = pl.ds(level + 1 - CHUNK, CHUNK)
            for i, hbm in enumerate((zonal_hbm, meridional_hbm, theta_hbm)):
                store = pltpu.make_async_copy(out.at[i, done], hbm.at[done], sem.at[i, level // CHUNK])
                store.start()
                stores.append(store)
    for store in stores:
        store.wait()


def on_device(nlon, nlat, *fields):
    levels, rows, columns = fields[0].shape
    assert (levels, columns) == (8, LANES)
    f32 = jnp.float32
    length = 2 * EDGE + levels + 2 * HALO
    high = rows + 2 * HALO
    block, padded = (levels, rows, LANES), (levels, rows + 2 * PAD, LANES)
    kept = [padded, (rows, LANES), block, padded, block, block]
    shapes = [
        padded, (2, length, LANES), (2, rows, LANES), (2, 2, 2 * HALO, LANES), (2, rows, LANES), (2, length, LANES),
        (4, high, LANES), (6, levels, rows + 2 * PAD, LANES), padded,
    ]
    held = pl.pallas_call(
        functools.partial(kernel, nlon, nlat),
        out_shape=[pltpu.VMEM(shape, f32) for shape in kept],
        in_specs=[pl.BlockSpec(memory_space=pl.ANY)] * 5,
        out_specs=[pl.BlockSpec(memory_space=pltpu.VMEM)] * 6,
        scratch_shapes=[pltpu.VMEM(shape, f32) for shape in shapes]
        + [pltpu.SemaphoreType.DMA((5,)), pltpu.SemaphoreType.DMA((8,)), pltpu.SemaphoreType.DMA((8,))],
        compiler_params=pltpu.CompilerParams(collective_id=0, has_side_effects=True),
        name="halo_step",
    )(*fields)
    held = [pltpu.with_memory_space_constraint(x, pltpu.VMEM) for x in held]
    outputs = pl.pallas_call(
        finish_kernel,
        out_shape=[jax.ShapeDtypeStruct(block, f32)] * 4,
        in_specs=[pl.BlockSpec(memory_space=pltpu.VMEM)] * 6,
        out_specs=[pl.BlockSpec(memory_space=pl.ANY)] * 4,
        scratch_shapes=[
            pltpu.VMEM((3, levels, rows, LANES), f32),
            pltpu.SemaphoreType.DMA((4, levels // CHUNK)),
        ],
        name="finish",
    )(*held)
    return tuple(outputs)


def solution(mesh):
    spec = P(None, "lat", "lon")
    return jax.shard_map(
        functools.partial(on_device, mesh.shape["lon"], mesh.shape["lat"]),
        mesh=mesh,
        in_specs=(spec,) * 5,
        out_specs=(spec,) * 4,
        check_vma=False,
    )
```

```python
import functools

import jax
import jax.numpy as jnp
from jax import lax
from jax.experimental import pallas as pl
from jax.experimental.pallas import tpu as pltpu
from jax.sharding import PartitionSpec as P

SWEEPS = 3
HALO = SWEEPS + 1
CHUNK = 4
LANES = 128
PAD = 8
EDGE = 8 * HALO
MESH = pl.DeviceIdType.MESH

divergence_weight = 0.5
thermal_weight = 0.3
vertical_coupling = 0.5
gradient_weight = 0.5
adjust_weight = 0.5


def lane_of(rows):
    return lax.broadcasted_iota(jnp.int32, (rows, LANES), 1)


def turn(x, shift, axis=1):
    shift = shift % x.shape[axis]
    return x if shift == 0 else pltpu.roll(x, shift, axis)


def kernel(
    nlon, nlat, u_hbm, v_hbm, t_hbm, p_hbm, k_hbm,
    xb, side_ref, u_ref, v_tall, t_ref, p_ref,
    k_tall, ns_ref, ew_ref, cn_ref, own_ref, ns_send,
    tall, coef, xa, load_sem, send_sem, recv_sem,
):
    levels, rows, _ = t_ref.shape
    lon, lat = lax.axis_index("lon"), lax.axis_index("lat")
    poles = (lat == 0, lat == nlat - 1)

    def partner(side, shift):
        pole = poles[side]
        row = jnp.where(pole, lat, lat + (1 if side else -1))
        col = lax.rem(lon + shift + nlon + jnp.where(pole, nlon // 2, 0), nlon)
        return {"lon": col, "lat": row}

    def beside(shift):
        return {"lon": lax.rem(lon + shift + nlon, nlon), "lat": lat}

    everyone = [beside(-1), beside(1)]
    everyone += [partner(side, shift) for side in (0, 1) for shift in (-1, 0, 1)]
    barrier = pltpu.get_barrier_semaphore()
    for device in everyone:
        pl.semaphore_signal(barrier, inc=1, device_id=device, device_id_type=MESH)

    loads = [
        pltpu.make_async_copy(src, dst, load_sem.at[i])
        for i, (src, dst) in enumerate((
            (k_hbm, k_tall.at[:, pl.ds(PAD, rows)]), (u_hbm, u_ref),
            (v_hbm, v_tall.at[:, pl.ds(PAD, rows)]), (t_hbm, t_ref), (p_hbm, p_ref),
        ))
    ]
    for load in loads:
        load.start()
    inner = slice(PAD, PAD + rows)
    lane = lane_of(rows)
    group = lane // HALO
    row_id = lax.broadcasted_iota(jnp.int32, (rows, LANES), 0)
    place = [[jnp.where(poles[s], HALO - 1 - r, r) for r in range(HALO)] for s in (0, 1)]
    first = (0, rows - HALO)
    signs = [jnp.where(poles[s], -1.0, 1.0).astype(jnp.float32) for s in (0, 1)]
    west = jnp.zeros((rows, LANES), jnp.float32)
    east = jnp.zeros((rows, LANES), jnp.float32)

    def packed(pair, field, index, level):
        slot = index * levels + level
        moved = turn(field, (slot + 1) * HALO)
        west, east = pair
        return (
            jnp.where(group == (slot + 1) % (LANES // HALO), moved, west),
            jnp.where(group == slot, moved, east),
        )

    pair = (west, east)
    for index, ref, load in ((1, k_tall, loads[0]), (2, u_ref, loads[1]), (3, v_tall, loads[2])):
        load.wait()
        for level in range(levels):
            pair = packed(pair, ref[level] if ref is u_ref else ref[level, inner], index, level)
    loads[3].wait()
    loads[4].wait()
    for level in range(levels):
        u, v = u_ref[level], v_tall[level, inner]
        u_diff = jnp.where(lane == LANES - 1, 0.0, turn(u, -1)) - jnp.where(lane == 0, 0.0, turn(u, 1))
        v_diff = jnp.where(row_id == rows - 1, 0.0, turn(v, -1, 0)) - jnp.where(row_id == 0, 0.0, turn(v, 1, 0))
        part = p_ref[level] - 0.5 * divergence_weight * (u_diff + v_diff) + thermal_weight * t_ref[level]
        xa[level, inner] = part
        pair = packed(pair, part, 0, level)
    west, east = pair
    west = turn(west, -HALO)
    own_ref[0] = west
    own_ref[1] = east
    base = 2 * EDGE + levels
    for s in (0, 1):
        flip = jnp.where(lane_of(1) >= 3 * EDGE, signs[s], 1.0)
        for r in range(HALO):
            here = slice(first[s] + r, first[s] + r + 1)
            ns_send[s, pl.ds(base + place[s][r], 1)] = west[here] * flip
            ns_send[s, pl.ds(base + HALO + place[s][r], 1)] = east[here] * flip

    for s in (0, 1):
        for level in range(levels):
            for r in range(HALO):
                here = slice(PAD + first[s] + r, PAD + first[s] + r + 1)
                ns_send[s, pl.ds(level * HALO + place[s][r], 1)] = xa[level, here]
                ns_send[s, pl.ds(EDGE + level * HALO + place[s][r], 1)] = k_tall[level, here]
            edge = PAD if s == 0 else PAD + rows - 1
            ns_send[s, 2 * EDGE + level : 2 * EDGE + level + 1] = v_tall[level, edge : edge + 1] * signs[s]
    pl.semaphore_wait(barrier, len(everyone))
    copies = []

    def send(src, dst, device, out, into):
        copy = pltpu.make_async_remote_copy(
            src_ref=src, dst_ref=dst, send_sem=send_sem.at[out], recv_sem=recv_sem.at[into],
            device_id=device, device_id_type=MESH,
        )
        copy.start()
        copies.append(copy)

    def arrive(dst, into):
        pltpu.make_async_remote_copy(
            src_ref=dst, dst_ref=dst, send_sem=send_sem.at[0], recv_sem=recv_sem.at[into],
            device_id=beside(1), device_id_type=MESH,
        ).wait_recv()

    send(own_ref.at[0], ew_ref.at[1], beside(-1), 0, 1)
    send(own_ref.at[1], ew_ref.at[0], beside(1), 1, 0)
    there = [jnp.where(poles[s], s, 1 - s) for s in (0, 1)]
    for s in (0, 1):
        send(ns_send.at[s], ns_ref.at[there[s]], partner(s, 0), 2 + s, 2 + there[s])
    for s in (0, 1):
        corner = ns_send.at[s, pl.ds(base, 2 * HALO)]
        send(corner, cn_ref.at[there[s], 1], partner(s, -1), 4 + 2 * s, 4 + 2 * there[s] + 1)
        send(corner, cn_ref.at[there[s], 0], partner(s, 1), 5 + 2 * s, 4 + 2 * there[s])

    high = rows + 2 * HALO
    core = slice(HALO, HALO + rows)
    top = HALO + rows
    bottom = PAD - HALO
    zero_row = jnp.zeros((1, LANES), jnp.float32)

    def weigh(level, start, count):
        at = lambda shift: slice(start + shift, start + shift + count)
        k = k_tall[level, at(0)]
        ke = 0.5 * (k + turn(k, -1))
        kw = 0.5 * (k + turn(k, 1))
        kn = 0.5 * (k + k_tall[level, at(1)])
        ks = 0.5 * (k + k_tall[level, at(-1)])
        vertical = vertical_coupling * ((level > 0) + (level < levels - 1))
        inv = 1.0 / (1.0 + ke + kw + kn + ks + vertical)
        found = (xa[level, at(0)] * inv, ke * inv, kw * inv, kn * inv, ks * inv, vertical_coupling * inv)
        for index, value in enumerate(found):
            coef[index, level, at(0)] = value

    for level in range(levels):
        for ref in (xa, xb, k_tall):
            ref[level, bottom - 1 : bottom] = zero_row
            ref[level, bottom + high : bottom + high + 1] = zero_row
        for start in (bottom, PAD + rows):
            k_tall[level, start : start + HALO] = jnp.zeros((HALO, LANES), jnp.float32)
        weigh(level, PAD, rows)

    for side in (0, 1):
        arrive(ns_ref.at[side], 2 + side)
    for level in range(levels):
        for s, start in ((0, bottom), (1, PAD + rows)):
            xa[level, start : start + HALO] = ns_ref[s, level * HALO : (level + 1) * HALO]
            k_tall[level, start : start + HALO] = ns_ref[s, EDGE + level * HALO : EDGE + (level + 1) * HALO]
        for s, (outer, inside) in enumerate(((PAD - 1, PAD), (PAD + rows, PAD + rows - 1))):
            sign = 0.25 if s == 0 else -0.25
            beyond_v = ns_ref[s, 2 * EDGE + level : 2 * EDGE + level + 1]
            xa[level, outer : outer + 1] = xa[level, outer : outer + 1] - sign * v_tall[level, inside : inside + 1]
            xa[level, inside : inside + 1] = xa[level, inside : inside + 1] + sign * beyond_v
        for start in (bottom, PAD + rows - HALO):
            weigh(level, start, 2 * HALO)
    for side in (0, 1):
        arrive(ew_ref.at[side], side)
        arrive(cn_ref.at[side, 0], 4 + 2 * side)
        arrive(cn_ref.at[side, 1], 5 + 2 * side)

    tall[0, core], tall[1, core] = ew_ref[0], own_ref[0]
    tall[2, core], tall[3, core] = own_ref[1], ew_ref[1]
    for s in (0, 1):
        rim = slice(0, HALO) if s == 0 else slice(top, high)
        tall[0, rim] = cn_ref[s, 0, HALO : 2 * HALO]
        tall[1, rim] = ns_ref[s, base : base + HALO]
        tall[2, rim] = ns_ref[s, base + HALO : base + 2 * HALO]
        tall[3, rim] = cn_ref[s, 1, :HALO]

    lane = lane_of(high)
    part, column = lane // EDGE, lane % HALO
    level_id = (lane % EDGE) // HALO
    row_id = lax.broadcasted_iota(jnp.int32, (high, LANES), 0)
    parts = [tall[i] for i in range(4)]

    def side_field(index):
        moved = [turn(parts[i], (i - index) * EDGE) for i in range(4)]
        return jnp.where(part < 2, jnp.where(part == 0, moved[0], moved[1]), jnp.where(part == 2, moved[2], moved[3]))

    def side_east(x):
        return jnp.where(column == HALO - 1, turn(x, HALO - 1 - EDGE), turn(x, -1))

    def side_west(x):
        return jnp.where(column == 0, turn(x, EDGE - HALO + 1), turn(x, 1))

    def fix_rows(partial, v):
        lack_north = (row_id == HALO - 1) | (row_id == top - 1)
        lack_south = (row_id == HALO) | (row_id == top)
        return partial - jnp.where(lack_north, 0.25 * turn(v, -1, 0), 0.0) + jnp.where(lack_south, 0.25 * turn(v, 1, 0), 0.0)

    side_p, side_k, side_u, side_v = [side_field(i) for i in range(4)]
    lack_east = (column == HALO - 1) & (part % 2 == 0)
    lack_west = (column == 0) & (part % 2 == 1)
    side_s = side_p - jnp.where(lack_east, 0.25 * side_east(side_u), 0.0) + jnp.where(lack_west, 0.25 * side_west(side_u), 0.0)
    side_s = fix_rows(side_s, side_v)
    se = 0.5 * (side_k + side_east(side_k))
    sw = 0.5 * (side_k + side_west(side_k))
    sn = 0.5 * (side_k + turn(side_k, -1, 0))
    ss = 0.5 * (side_k + turn(side_k, 1, 0))
    rim_level = (level_id == 0) | (level_id == levels - 1)
    inverse = 1.0 / (1.0 + se + sw + sn + ss + jnp.where(rim_level, vertical_coupling, 2.0 * vertical_coupling))
    se, sw, sn, ss = se * inverse, sw * inverse, sn * inverse, ss * inverse
    s0 = side_s * inverse
    up = jnp.where(level_id == levels - 1, 0.0, vertical_coupling * inverse)
    down = jnp.where(level_id == 0, 0.0, vertical_coupling * inverse)
    side = [side_s]
    for _ in range(SWEEPS):
        x = side[-1]
        side.append(
            s0 + se * side_east(x) + sw * side_west(x) + sn * turn(x, -1, 0) + ss * turn(x, 1, 0)
            + up * turn(x, -HALO) + down * turn(x, HALO)
        )

    rims = [jnp.where(column == HALO - 1, turn(x, -(EDGE + HALO)), x) for x in side]
    edge = (lane == 0) | (lane == LANES - 1)

    def with_edges(x, step, level):
        return jnp.where(edge, turn(rims[step], -(EDGE + level * HALO)), x)

    here = slice(bottom, bottom + high)
    north, south = slice(bottom + 1, bottom + 1 + high), slice(bottom - 1, bottom - 1 + high)
    for level in range(levels):
        xa[level, here] = with_edges(xa[level, here], 0, level)

    now, later = xa, xb
    for sweep in range(SWEEPS):
        for level in range(levels):
            x = now[level, here]
            if level == 0:
                column_sum = now[1, here]
            elif level == levels - 1:
                column_sum = now[level - 1, here]
            else:
                column_sum = now[level + 1, here] + now[level - 1, here]
            value = (
                coef[0, level, here]
                + coef[1, level, here] * turn(x, -1)
                + coef[2, level, here] * turn(x, 1)
                + coef[3, level, here] * now[level, north]
                + coef[4, level, here] * now[level, south]
                + coef[5, level, here] * column_sum
            )
            later[level, here] = with_edges(value, sweep + 1, level)
        now, later = later, now

    side_ref[...] = side[SWEEPS][core]
    for copy in copies:
        copy.wait_send()


def east_west_of(x, beyond, level, lane):
    east = jnp.where(lane == LANES - 1, turn(beyond, LANES - 1 - 3 * EDGE - level * HALO), turn(x, -1))
    west = jnp.where(lane == 0, turn(beyond, -(level * HALO + HALO - 1)), turn(x, 1))
    return east, west


def finish_kernel(
    x_ref, side_ref, u_ref, v_tall, t_ref, p_ref,
    zonal_hbm, meridional_hbm, theta_hbm, next_hbm, out, sem,
):
    levels, rows, _ = u_ref.shape
    lane = lane_of(rows)
    beyond = side_ref[...]
    stores = [pltpu.make_async_copy(x_ref.at[:, pl.ds(PAD, rows)], next_hbm, sem.at[3, 0])]
    stores[0].start()
    for level in range(levels):
        x = x_ref[level, PAD : PAD + rows]
        east, west = east_west_of(x, beyond, level, lane)
        north_south = x_ref[level, PAD + 1 : PAD + 1 + rows] - x_ref[level, PAD - 1 : PAD - 1 + rows]
        out[0, level] = u_ref[level] - 0.5 * gradient_weight * (east - west)
        out[1, level] = v_tall[level, PAD : PAD + rows] - 0.5 * gradient_weight * north_south
        out[2, level] = t_ref[level] - adjust_weight * (x - p_ref[level])
        if (level + 1) % CHUNK == 0:
            done = pl.ds(level + 1 - CHUNK, CHUNK)
            for i, hbm in enumerate((zonal_hbm, meridional_hbm, theta_hbm)):
                store = pltpu.make_async_copy(out.at[i, done], hbm.at[done], sem.at[i, level // CHUNK])
                store.start()
                stores.append(store)
    for store in stores:
        store.wait()


def on_device(nlon, nlat, *fields):
    levels, rows, columns = fields[0].shape
    assert (levels, columns) == (8, LANES)
    f32 = jnp.float32
    length = 2 * EDGE + levels + 2 * HALO
    high = rows + 2 * HALO
    block, padded = (levels, rows, LANES), (levels, rows + 2 * PAD, LANES)
    kept = [padded, (rows, LANES), block, padded, block, block]
    shapes = [
        padded, (2, length, LANES), (2, rows, LANES), (2, 2, 2 * HALO, LANES), (2, rows, LANES), (2, length, LANES),
        (4, high, LANES), (6, levels, rows + 2 * PAD, LANES), padded,
    ]
    held = pl.pallas_call(
        functools.partial(kernel, nlon, nlat),
        out_shape=[pltpu.VMEM(shape, f32) for shape in kept],
        in_specs=[pl.BlockSpec(memory_space=pl.ANY)] * 5,
        out_specs=[pl.BlockSpec(memory_space=pltpu.VMEM)] * 6,
        scratch_shapes=[pltpu.VMEM(shape, f32) for shape in shapes]
        + [pltpu.SemaphoreType.DMA((5,)), pltpu.SemaphoreType.DMA((8,)), pltpu.SemaphoreType.DMA((8,))],
        compiler_params=pltpu.CompilerParams(collective_id=0, has_side_effects=True),
        name="halo_step",
    )(*fields)
    held = [pltpu.with_memory_space_constraint(x, pltpu.VMEM) for x in held]
    outputs = pl.pallas_call(
        finish_kernel,
        out_shape=[jax.ShapeDtypeStruct(block, f32)] * 4,
        in_specs=[pl.BlockSpec(memory_space=pltpu.VMEM)] * 6,
        out_specs=[pl.BlockSpec(memory_space=pl.ANY)] * 4,
        scratch_shapes=[
            pltpu.VMEM((3, levels, rows, LANES), f32),
            pltpu.SemaphoreType.DMA((4, levels // CHUNK)),
        ],
        name="finish",
    )(*held)
    return tuple(outputs)


def solution(mesh):
    spec = P(None, "lat", "lon")
    return jax.shard_map(
        functools.partial(on_device, mesh.shape["lon"], mesh.shape["lat"]),
        mesh=mesh,
        in_specs=(spec,) * 5,
        out_specs=(spec,) * 4,
        check_vma=False,
    )
```
